128 devices in a mesh: row: 16 (over y, x), col: 8 (over z, core).
Axes of the slice: x: 4, y: 4, z: 4, core: 2. Of those that a mesh axis runs over, the one named last changes fastest.
Arguments:
- row_emb: float32 [128, 300, 1024], P(('row', 'col')), may hold values from -1.5 to 1.5
- col_emb: float32 [128, 300, 1024], P(('row', 'col')), may hold values from -1.5 to 1.5
- row_acc: float32 [128, 300, 1024], P(('row', 'col')), may hold values from 0.5 to 8
- col_acc: float32 [128, 300, 1024], P(('row', 'col')), may hold values from 0.5 to 8
- marginal_log: float32 [131072], replicated, may hold values from -2 to 1
- tile_rows: int32 [384], P(('row', 'col')), may hold values from 0 to 127, as said below
- tile_cols: int32 [384], P(('row', 'col')), may hold values from 0 to 127, as said below
- counts: int32 [384, 1024, 1024], P(('row', 'col')), may hold values from 0 to 2047
Outputs:
- new_row_emb: float32 [128, 300, 1024], P(('row', 'col'))
- new_col_emb: float32 [128, 300, 1024], P(('row', 'col'))
- new_row_acc: float32 [128, 300, 1024], P(('row', 'col'))
- new_col_acc: float32 [128, 300, 1024], P(('row', 'col'))
The draws below stay inside these ranges and needn't reach their ends.
Inputs may be any that keep to these rules, and one draw needn't show every extreme that they name: Block g of the embeddings lies on device g in the mesh's order (row slowest). Slot k lies on device p = k // 3; with p at row index r and col index c, tile_rows[k] // 8 equals r. With slot k on the device at col index c, tile_cols[k] % 8 equals c.
All inputs are finite; a program needn't handle non-finite values.
Results may differ from the reference program's by a relative error of at most 0.019.
Values may be sent and summed in bfloat16 or wider, within the bound.
No kernel may reach another device: no remote copies, remote signals or barrier semaphores. Data moves between devices by JAX's collectives and lax.ppermute only.
A program may use at most 128 MiB of HBM per device.

```python
import math
import jax
import jax.numpy as jnp
from jax import lax

D = 300
BLOCK = 1024
TILES_DEV = 3
NBLK = 128
TILES = 384
WORDS = 131072
N_ROW = 16
N_COL = 8


def pick_skewed(key, choices_total, shape_tuple):
    ranks = jnp.arange(choices_total, dtype=jnp.int32)
    weights = jnp.maximum(1, 64 // (ranks + 1))
    bounds = jnp.cumsum(weights)
    picks = jax.random.randint(key, shape_tuple, 0, bounds[-1])
    rank_of = jnp.sum((picks[..., None] >= bounds).astype(jnp.int32), axis=-1)
    ordering = jax.random.permutation(jax.random.fold_in(key, 7), choices_total)
    return ordering[rank_of].astype(jnp.int32)


def draw_tile_rows(key, part):
    slots = jnp.arange(TILES, dtype=jnp.int32)
    device = slots // TILES_DEV
    row_index = device // N_COL
    chosen = pick_skewed(jax.random.fold_in(key, 11), N_COL, (TILES,))
    return (row_index * N_COL + chosen).astype(jnp.int32)


def draw_tile_cols(key, part):
    slots = jnp.arange(TILES, dtype=jnp.int32)
    device = slots // TILES_DEV
    col_index = device % N_COL
    chosen = pick_skewed(jax.random.fold_in(key, 13), N_ROW, (TILES,))
    return (chosen * N_COL + col_index).astype(jnp.int32)


def draw_counts(key, part):
    shape_tuple = (TILES, BLOCK, BLOCK)
    present = jax.random.randint(jax.random.fold_in(key, 21), shape_tuple, 0, 5) >= 2
    level = jax.random.randint(jax.random.fold_in(key, 22), shape_tuple, 0, 12)
    raw_bits = jax.random.randint(jax.random.fold_in(key, 23), shape_tuple, 0, 1 << 20)
    values = 1 + raw_bits % jnp.left_shift(jnp.ones(shape_tuple, jnp.int32), level)
    values = jnp.minimum(values, 2047)
    return jnp.where(present, values, 0).astype(jnp.int32)


def block_levels(key, shape, split, smallest, top_value):
    def one(axis_at, parts):
        draws = jax.random.uniform(jax.random.fold_in(jax.random.fold_in(key, 6), axis_at), (parts,), jnp.float32, smallest / len(split), top_value / len(split))
        return jnp.repeat(jnp.exp(draws), shape[axis_at] // parts).reshape((-1,) + (1,) * (len(shape) - axis_at - 1))

    gain = one(*split[0])
    for cut in split[1:]:
        gain = gain * one(*cut)
    return gain


def normal_values(own_key, dims, spread, reach, shards=(), kind=jnp.bfloat16):
    values = spread * jax.random.normal(own_key, dims, jnp.float32)
    if shards:
        values = values * block_levels(own_key, dims, shards, -0.22, 0.18)
    return jnp.clip(values, -reach, reach).astype(kind)


def setup_inputs(seed: int = 0) -> dict:
    key_list = jax.random.split(jax.random.key(seed), 9)
    row_emb = normal_values(key_list[0], (NBLK, D, BLOCK), 0.25, 1.5, ((0, 128),), jnp.float32)
    col_emb = normal_values(key_list[1], (NBLK, D, BLOCK), 0.25, 1.5, ((0, 128),), jnp.float32)
    row_acc = jnp.clip(jnp.exp(math.log(8.0) - 2.7725887 * jax.random.uniform(key_list[2], (NBLK, D, BLOCK), jnp.float32) ** block_levels(key_list[2], (NBLK, D, BLOCK), ((0, 128),), -0.2, 0.2)), 0.5, 8.0)
    col_acc = jnp.clip(jnp.exp(math.log(8.0) - 2.7725887 * jax.random.uniform(key_list[3], (NBLK, D, BLOCK), jnp.float32) ** block_levels(key_list[3], (NBLK, D, BLOCK), ((0, 128),), -0.2, 0.2)), 0.5, 8.0)
    marginal_log = jnp.clip(jax.random.uniform(key_list[4], (WORDS,), jnp.float32, -2.0, 1.0), -2.0, 1.0)
    tile_rows = draw_tile_rows(jax.random.fold_in(key_list[8], 71), 0)
    tile_cols = draw_tile_cols(jax.random.fold_in(key_list[8], 71), 0)
    counts = draw_counts(jax.random.fold_in(key_list[8], 71), 0)
    return dict(row_emb=row_emb, col_emb=col_emb, row_acc=row_acc, col_acc=col_acc, marginal_log=marginal_log, tile_rows=tile_rows, tile_cols=tile_cols, counts=counts)


err_scale = 0.03125
learn_rate = 0.1

def tile_terms(row_block, col_block, tile_counts, row_margin, col_margin):
    scores = lax.dot_general(row_block, col_block, (((0,), (0,)), ((), ())), preferred_element_type=jnp.float32)
    counted = tile_counts.astype(jnp.float32)
    shifted_log = jnp.log(jnp.maximum(counted, 1.0)) - row_margin[:, None] - col_margin[None, :]
    residue = scores - shifted_log
    weighted = (0.1 + 0.25 * jnp.sqrt(counted)) * residue
    cell_grad = jnp.where(tile_counts > 0, weighted, jax.nn.sigmoid(residue)) * err_scale
    errors = cell_grad.astype(jnp.bfloat16)
    row_term = lax.dot_general(col_block, errors, (((1,), (1,)), ((), ())), preferred_element_type=jnp.float32)
    col_term = jnp.dot(row_block, errors, preferred_element_type=jnp.float32)
    return (row_term, col_term)

def add_slot(buffer, slot_index, term):
    old_value = lax.dynamic_index_in_dim(buffer, slot_index, 0, keepdims=False)
    return lax.dynamic_update_index_in_dim(buffer, old_value + term, slot_index, 0)

def adagrad(weights, history, gradient):
    grown = history + gradient * gradient
    return (weights - learn_rate * gradient / jnp.sqrt(grown), grown)

def reference(row_emb, col_emb, row_acc, col_acc, marginal_log, tile_rows, tile_cols, counts):
    row_low = row_emb.astype(jnp.bfloat16)
    col_low = col_emb.astype(jnp.bfloat16)
    col_grid = col_low.reshape(N_ROW, N_COL, D, BLOCK)
    zeros_table = jnp.zeros((NBLK, D, BLOCK), jnp.float32)

    def device_step(tables, device):
        row_table, col_table = tables
        row_index = (device // N_COL).astype(jnp.int32)
        col_index = (device % N_COL).astype(jnp.int32)
        rows_near = lax.dynamic_slice_in_dim(row_low, row_index * N_COL, N_COL, 0)
        cols_near = lax.dynamic_index_in_dim(col_grid, col_index, 1, keepdims=False)
        row_part = jnp.zeros((N_COL, D, BLOCK), jnp.float32)
        col_part = jnp.zeros((N_ROW, D, BLOCK), jnp.float32)
        for tile_slot in range(TILES_DEV):
            position = (device * TILES_DEV + tile_slot).astype(jnp.int32)
            row_id = lax.dynamic_index_in_dim(tile_rows, position, 0, keepdims=False).astype(jnp.int32)
            col_id = lax.dynamic_index_in_dim(tile_cols, position, 0, keepdims=False).astype(jnp.int32)
            row_slot = (row_id - row_index * N_COL).astype(jnp.int32)
            col_slot = (col_id // N_COL).astype(jnp.int32)
            row_block = lax.dynamic_index_in_dim(rows_near, row_slot, 0, keepdims=False)
            col_block = lax.dynamic_index_in_dim(cols_near, col_slot, 0, keepdims=False)
            tile_counts = lax.dynamic_index_in_dim(counts, position, 0, keepdims=False)
            row_margin = lax.dynamic_slice_in_dim(marginal_log, (row_id * BLOCK).astype(jnp.int32), BLOCK)
            col_margin = lax.dynamic_slice_in_dim(marginal_log, (col_id * BLOCK).astype(jnp.int32), BLOCK)
            row_term, col_term = tile_terms(row_block, col_block, tile_counts, row_margin, col_margin)
            row_part = add_slot(row_part, row_slot, row_term)
            col_part = add_slot(col_part, col_slot, col_term)
        row_round = lax.optimization_barrier(row_part.astype(jnp.bfloat16)).astype(jnp.float32)
        col_round = lax.optimization_barrier(col_part.astype(jnp.bfloat16)).astype(jnp.float32)
        old_rows = lax.dynamic_slice_in_dim(row_table, row_index * N_COL, N_COL, 0)
        row_table = lax.dynamic_update_slice_in_dim(row_table, old_rows + row_round, row_index * N_COL, 0)
        col_gridded = col_table.reshape(N_ROW, N_COL, D, BLOCK)
        old_cols = lax.dynamic_index_in_dim(col_gridded, col_index, 1, keepdims=False)
        col_gridded = lax.dynamic_update_index_in_dim(col_gridded, old_cols + col_round, col_index, 1)
        return ((row_table, col_gridded.reshape(NBLK, D, BLOCK)), None)
    sums_pair, unused = lax.scan(device_step, (zeros_table, zeros_table), jnp.arange(NBLK, dtype=jnp.int32))
    row_grad, col_grad = sums_pair
    new_row_emb, new_row_acc = adagrad(row_emb, row_acc, row_grad)
    new_col_emb, new_col_acc = adagrad(col_emb, col_acc, col_grad)
    return (new_row_emb, new_col_emb, new_row_acc, new_col_acc)
```

```python
import jax
import jax.numpy as jnp
from jax import lax
from jax.experimental import pallas as pl
from jax.experimental.pallas import tpu as pltpu
from jax.sharding import PartitionSpec as P

err_scale = 0.03125
learn_rate = 0.1

DIM = 300
PAD = 304
HALF = 152
META = 160
BLOCK = 1024
LANES = 128
PARTS = 16
TILES = 3
COLS = 8
CHUNK = 256

f32 = jnp.float32
bf16 = jnp.bfloat16


def prep_kernel(wanted, row_ref, col_ref, low_ref, slice_ref):
    low_ref[0, 288:PAD, :] = jnp.zeros((16, BLOCK), bf16)
    low_ref[0, 0:DIM, :] = row_ref[0].astype(bf16)
    lane = lax.broadcasted_iota(jnp.int32, (8, LANES), 1)
    spot = lax.broadcasted_iota(jnp.int32, (8, LANES), 0)
    ask = [wanted[t] // COLS for t in range(TILES)]
    meta = jnp.where(lane == 0, ask[0], jnp.where(lane == 1, ask[1], ask[2])).astype(f32)
    for n in range(BLOCK // LANES):
        cut = slice(n * LANES, (n + 1) * LANES)
        top = jnp.concatenate([col_ref[0, 0:HALF, cut], meta], axis=0)
        slice_ref[2 * n] = top.astype(bf16)
        last = pltpu.roll(col_ref[0, DIM - 8 : DIM, cut], 4, 0)
        last = jnp.where(spot < 4, last, 0.0)
        low = jnp.concatenate([col_ref[0, HALF : DIM - 4, cut], last, meta], axis=0)
        slice_ref[2 * n + 1] = low.astype(bf16)


def prep(tile_cols, row_emb, col_emb):
    return pl.pallas_call(
        prep_kernel,
        out_shape=(
            jax.ShapeDtypeStruct((1, PAD, BLOCK), bf16),
            jax.ShapeDtypeStruct((PARTS, META, LANES), bf16),
        ),
        in_specs=[
            pl.BlockSpec(memory_space=pltpu.SMEM),
            pl.BlockSpec(memory_space=pltpu.VMEM),
            pl.BlockSpec(memory_space=pltpu.VMEM),
        ],
        name="prep",
    )(tile_cols, row_emb, col_emb)


def pick_kernel(held_ref, out_ref, meta_ref, asked, sem):
    for d in range(PARTS):
        meta_ref[d : d + 1, :] = held_ref[d, HALF:META, :].astype(f32)[0:1, :].astype(jnp.int32)
    move = pltpu.make_async_copy(meta_ref, asked, sem)
    move.start()
    move.wait()
    for d in range(PARTS):
        for t in range(TILES):
            out_ref[d, t] = held_ref[asked[d, t], 0:HALF, :]


def pick(held):
    return pl.pallas_call(
        pick_kernel,
        out_shape=(
            jax.ShapeDtypeStruct((PARTS, TILES, HALF, LANES), bf16),
            jax.ShapeDtypeStruct((PARTS, LANES), jnp.int32),
        ),
        in_specs=[pl.BlockSpec(memory_space=pltpu.VMEM)],
        scratch_shapes=[pltpu.SMEM((PARTS, LANES), jnp.int32), pltpu.SemaphoreType.DMA],
        name="pick",
    )(held)


def tile_kernel(
    rows, cols, part_ref, near_ref, count_ref, row_margin_ref, col_margin_ref,
    col_out_ref, row_out_ref, col_block, row_terms, col_term,
):
    t = pl.program_id(0)

    @pl.when(t == 0)
    def _():
        row_out_ref[...] = jnp.zeros((COLS, PAD, BLOCK), bf16)

    for s in range(PARTS):
        n, h = s // 2, s % 2
        col_block[h * HALF : (h + 1) * HALF, n * LANES : (n + 1) * LANES] = part_ref[s, 0]
    row_margin = jnp.transpose(row_margin_ref[0])
    col_margin = jnp.concatenate(
        [col_margin_ref[0, n : n + 1, :] for n in range(BLOCK // LANES)], axis=1
    )
    for c in range(BLOCK // CHUNK):
        cut = slice(c * CHUNK, (c + 1) * CHUNK)
        row_part = near_ref[0, :, cut]
        scores = lax.dot_general(
            row_part, col_block[...], (((0,), (0,)), ((), ())), preferred_element_type=f32
        )
        margin = jnp.concatenate(
            [row_margin[:, n : n + 1] for n in range(2 * c, 2 * c + 2)], axis=0
        )
        counted = count_ref[0, cut, :].astype(f32)
        capped = jnp.maximum(counted, 1.0)
        residue = scores - jnp.log(capped) + (margin + col_margin)
        weight = (0.1 * err_scale) + (0.25 * err_scale) * (counted * lax.rsqrt(capped))
        logistic = (0.5 * err_scale) + (0.5 * err_scale) * jnp.tanh(0.5 * residue)
        errors = jnp.where(counted > 0.0, weight * residue, logistic).astype(bf16)
        row_terms[t, :, cut] = lax.dot_general(
            col_block[...], errors, (((1,), (1,)), ((), ())), preferred_element_type=f32
        )
        term = jnp.dot(row_part, errors, preferred_element_type=f32)
        if c == 0:
            col_term[...] = term
        else:
            col_term[...] += term
    for s in range(PARTS):
        n, h = s // 2, s % 2
        col_out_ref[s, 0] = col_term[
            h * HALF : (h + 1) * HALF, n * LANES : (n + 1) * LANES
        ].astype(bf16)

    @pl.when(t == TILES - 1)
    def _():
        slots = [rows[k] % COLS for k in range(TILES)]
        for k in range(TILES):
            total = row_terms[k]
            for other in range(TILES):
                if other != k:
                    same = jnp.where(slots[other] == slots[k], 1.0, 0.0)
                    total = total + same * row_terms[other]
            row_out_ref[slots[k]] = total.astype(bf16)


def tile_terms(tile_rows, tile_cols, parts, near, counts, margins):
    grid_spec = pltpu.PrefetchScalarGridSpec(
        num_scalar_prefetch=2,
        grid=(TILES,),
        in_specs=[
            pl.BlockSpec((PARTS, 1, HALF, LANES), lambda t, rows, cols: (0, t, 0, 0)),
            pl.BlockSpec((1, PAD, BLOCK), lambda t, rows, cols: (rows[t] % COLS, 0, 0)),
            pl.BlockSpec((1, BLOCK, BLOCK), lambda t, rows, cols: (t, 0, 0)),
            pl.BlockSpec((1, 8, LANES), lambda t, rows, cols: (rows[t], 0, 0)),
            pl.BlockSpec((1, 8, LANES), lambda t, rows, cols: (cols[t], 0, 0)),
        ],
        out_specs=[
            pl.BlockSpec((PARTS, 1, HALF, LANES), lambda t, rows, cols: (0, t, 0, 0)),
            pl.BlockSpec((COLS, PAD, BLOCK), lambda t, rows, cols: (0, 0, 0)),
        ],
        scratch_shapes=[
            pltpu.VMEM((PAD, BLOCK), bf16),
            pltpu.VMEM((TILES, PAD, BLOCK), f32),
            pltpu.VMEM((PAD, BLOCK), f32),
        ],
    )
    return pl.pallas_call(
        tile_kernel,
        grid_spec=grid_spec,
        out_shape=(
            jax.ShapeDtypeStruct((PARTS, TILES, HALF, LANES), bf16),
            jax.ShapeDtypeStruct((COLS, PAD, BLOCK), bf16),
        ),
        compiler_params=pltpu.CompilerParams(
            dimension_semantics=("arbitrary",), vmem_limit_bytes=56 << 20
        ),
        name="tile_terms",
    )(tile_rows, tile_cols, parts, near, counts, margins, margins)


def owner_sum_kernel(asked, term_ref, out_ref, total):
    total[...] = jnp.zeros((PARTS, HALF, LANES), f32)
    for d in range(PARTS):
        for t in range(TILES):
            total[asked[d, t]] += term_ref[d, t].astype(f32)
    out_ref[...] = total[...].astype(bf16)


def owner_sum(asked, terms):
    return pl.pallas_call(
        owner_sum_kernel,
        out_shape=jax.ShapeDtypeStruct((PARTS, HALF, LANES), bf16),
        in_specs=[
            pl.BlockSpec(memory_space=pltpu.SMEM),
            pl.BlockSpec(memory_space=pltpu.VMEM),
        ],
        scratch_shapes=[pltpu.VMEM((PARTS, HALF, LANES), f32)],
        name="owner_sum",
    )(asked, terms)


def adagrad(weights, history, gradient):
    grown = history + gradient * gradient
    return (weights - learn_rate * gradient / jnp.sqrt(grown), grown)


def col_update_kernel(emb_ref, acc_ref, grad_ref, new_emb_ref, new_acc_ref):
    for n in range(BLOCK // LANES):
        cut = slice(n * LANES, (n + 1) * LANES)
        for h in range(2):
            length = HALF if h == 0 else DIM - HALF
            span = slice(h * HALF, h * HALF + length)
            new_emb_ref[0, span, cut], new_acc_ref[0, span, cut] = adagrad(
                emb_ref[0, span, cut],
                acc_ref[0, span, cut],
                grad_ref[2 * n + h].astype(f32)[0:length],
            )


def col_update(emb, acc, grad):
    shape = jax.ShapeDtypeStruct((1, DIM, BLOCK), f32)
    return pl.pallas_call(
        col_update_kernel,
        out_shape=(shape, shape),
        in_specs=[pl.BlockSpec(memory_space=pltpu.VMEM)] * 3,
        name="col_update",
    )(emb, acc, grad)


def body(row_emb, col_emb, row_acc, col_acc, marginal_log, tile_rows, tile_cols, counts):
    row_low, slices = prep(tile_cols, row_emb, col_emb)
    near = lax.all_gather(row_low, "col", axis=0, tiled=True)
    held = lax.all_to_all(slices, "row", 0, 0, tiled=True)
    picked, asked = pick(held)
    parts = lax.all_to_all(picked, "row", 0, 0, tiled=True)
    margins = marginal_log.reshape(-1, 8, LANES)
    col_terms, row_parts = tile_terms(tile_rows, tile_cols, parts, near, counts, margins)
    row_sum = lax.psum_scatter(row_parts, "col", scatter_dimension=0, tiled=True)
    terms = lax.all_to_all(col_terms, "row", 0, 0, tiled=True)
    sums = owner_sum(asked, terms)
    col_sum = lax.all_to_all(sums, "row", 0, 0, tiled=True)
    new_row_emb, new_row_acc = adagrad(row_emb, row_acc, row_sum[:, :DIM, :].astype(f32))
    new_col_emb, new_col_acc = col_update(col_emb, col_acc, col_sum)
    return (new_row_emb, new_col_emb, new_row_acc, new_col_acc)


def solution(mesh):
    block = P(("row", "col"), None, None)
    return jax.shard_map(
        body,
        mesh=mesh,
        in_specs=(block, block, block, block, P(), P(("row", "col")), P(("row", "col")), block),
        out_specs=(block, block, block, block),
        check_vma=False,
    )
```

```python
import jax
import jax.numpy as jnp
from jax import lax
from jax.experimental import pallas as pl
from jax.experimental.pallas import tpu as pltpu
from jax.sharding import PartitionSpec as P


err_scale = 0.03125
learn_rate = 0.1

DIM = 300
PAD = 304
HALF = 152
META = 160
BLOCK = 1024
LANES = 128
PARTS = 16
TILES = 3
COLS = 8
FIRST = 512
GROUPS = 8

f32 = jnp.float32
bf16 = jnp.bfloat16

SMEM = pl.BlockSpec(memory_space=pltpu.SMEM)
VMEM = pl.BlockSpec(memory_space=pltpu.VMEM)
HBM = pl.BlockSpec(memory_space=pl.ANY)


def span(first, length, n):
    return pl.ds(first * GROUPS + n, length, stride=GROUPS)


def cut_kernel(wanted, col_ref, slice_ref, col, sems):
    edge = HALF * GROUPS
    moves = [
        pltpu.make_async_copy(col_ref.at[:edge], col.at[:edge], sems.at[0]),
        pltpu.make_async_copy(col_ref.at[edge:], col.at[edge:], sems.at[1]),
    ]
    for move in moves:
        move.start()
    lane = lax.broadcasted_iota(jnp.int32, (8, LANES), 1)
    spot = lax.broadcasted_iota(jnp.int32, (8, LANES), 0)
    ask = [wanted[t] // COLS for t in range(TILES)]
    meta = jnp.where(lane == 0, ask[0], jnp.where(lane == 1, ask[1], ask[2])).astype(f32)
    moves[0].wait()
    for n in range(GROUPS):
        top = jnp.concatenate([col[span(0, HALF, n), :], meta], axis=0)
        slice_ref[2 * n] = top.astype(bf16)
    moves[1].wait()
    for n in range(GROUPS):
        last = pltpu.roll(col[span(DIM - 8, 8, n), :], 4, 0)
        last = jnp.where(spot < 4, last, 0.0)
        low = jnp.concatenate([col[span(HALF, DIM - 4 - HALF, n), :], last, meta], axis=0)
        slice_ref[2 * n + 1] = low.astype(bf16)


def cut_up(tile_cols, col_emb):
    return pl.pallas_call(
        cut_kernel,
        out_shape=jax.ShapeDtypeStruct((PARTS, META, LANES), bf16),
        in_specs=[SMEM, HBM],
        out_specs=VMEM,
        scratch_shapes=[pltpu.VMEM((DIM * GROUPS, LANES), f32), pltpu.SemaphoreType.DMA((2,))],
        compiler_params=pltpu.CompilerParams(vmem_limit_bytes=8 << 20),
        name="cut_up",
    )(tile_cols, col_emb)


def low_kernel(row_ref, low_ref):
    low_ref[0, 288:PAD, :] = jnp.zeros((16, BLOCK), bf16)
    for n in range(GROUPS):
        low_ref[0, 0:DIM, n * LANES : (n + 1) * LANES] = row_ref[span(0, DIM, n), :].astype(bf16)


def lower(row_emb):
    return pl.pallas_call(
        low_kernel,
        out_shape=jax.ShapeDtypeStruct((1, PAD, BLOCK), bf16),
        in_specs=[VMEM],
        out_specs=VMEM,
        compiler_params=pltpu.CompilerParams(vmem_limit_bytes=8 << 20),
        name="lower",
    )(row_emb)


def pick_kernel(held_ref, out_ref, meta_ref, picked, asked, sem, sems):
    for d in range(PARTS):
        meta_ref[d : d + 1, :] = held_ref[d, HALF:META, :].astype(f32)[0:1, :].astype(jnp.int32)
    move = pltpu.make_async_copy(meta_ref, asked, sem)
    move.start()
    move.wait()
    quarter = PARTS // 4
    moves = []
    for q in range(4):
        some = pl.ds(q * quarter, quarter)
        for d in range(q * quarter, (q + 1) * quarter):
            for t in range(TILES):
                picked[d, t] = held_ref[asked[d, t], 0:HALF, :]
        moves.append(pltpu.make_async_copy(picked.at[some], out_ref.at[some], sems.at[q]))
        moves[q].start()
    for move in moves:
        move.wait()


def pick(held):
    return pl.pallas_call(
        pick_kernel,
        out_shape=(
            pltpu.HBM((PARTS, TILES, HALF, LANES), bf16),
            jax.ShapeDtypeStruct((PARTS, LANES), jnp.int32),
        ),
        in_specs=[VMEM],
        out_specs=[HBM, VMEM],
        scratch_shapes=[
            pltpu.VMEM((PARTS, TILES, HALF, LANES), bf16),
            pltpu.SMEM((PARTS, LANES), jnp.int32),
            pltpu.SemaphoreType.DMA,
            pltpu.SemaphoreType.DMA((4,)),
        ],
        compiler_params=pltpu.CompilerParams(vmem_limit_bytes=8 << 20),
        name="pick",
    )(held)


def ready_kernel(
    rows, cols, count_ref, margin_ref, weight_ref, offset_ref, blank_ref, other_blank_ref,
    margin, zero, sems,
):
    t = pl.program_id(0)

    def margin_moves(k):
        return [
            pltpu.make_async_copy(margin_ref.at[rows[k]], margin.at[k, 0], sems.at[2 * k]),
            pltpu.make_async_copy(margin_ref.at[cols[k]], margin.at[k, 1], sems.at[2 * k + 1]),
        ]

    blank_moves = [
        pltpu.make_async_copy(zero, ref.at[s], sems.at[2 * TILES + 4 * i + s])
        for i, ref in enumerate((blank_ref, other_blank_ref))
        for s in range(4)
    ]

    @pl.when(t == 0)
    def _():
        for k in range(TILES):
            for move in margin_moves(k):
                move.start()
        zero[...] = jnp.zeros((PAD, BLOCK), bf16)
        for move in blank_moves:
            move.start()

    for move in margin_moves(t):
        move.wait()
    row_margin = jnp.transpose(margin[t, 0])
    col_margin = jnp.concatenate([margin[t, 1, n : n + 1, :] for n in range(GROUPS)], axis=1)
    for n in range(GROUPS):
        cut = slice(n * LANES, (n + 1) * LANES)
        counted = count_ref[0, cut, :].astype(f32)
        capped = jnp.maximum(counted, 1.0)
        offset_ref[0, cut, :] = (row_margin[:, n : n + 1] + col_margin) - jnp.log(capped)
        weight = (0.1 * err_scale) + (0.25 * err_scale) * (counted * lax.rsqrt(capped))
        weight_ref[0, cut, :] = jnp.where(counted > 0.0, weight, 0.0)

    @pl.when(t == TILES - 1)
    def _():
        for move in blank_moves:
            move.wait()


def ready(tile_rows, tile_cols, counts, margins):
    square = pl.BlockSpec((1, BLOCK, BLOCK), lambda t, *_: (t, 0, 0))
    grid_spec = pltpu.PrefetchScalarGridSpec(
        num_scalar_prefetch=2,
        grid=(TILES,),
        in_specs=[square, HBM],
        out_specs=[square, square, HBM, HBM],
        scratch_shapes=[
            pltpu.VMEM((TILES, 2, GROUPS, LANES), f32),
            pltpu.VMEM((PAD, BLOCK), bf16),
            pltpu.SemaphoreType.DMA((2 * TILES + 8,)),
        ],
    )
    return pl.pallas_call(
        ready_kernel,
        grid_spec=grid_spec,
        out_shape=(
            jax.ShapeDtypeStruct((TILES, BLOCK, BLOCK), f32),
            jax.ShapeDtypeStruct((TILES, BLOCK, BLOCK), f32),
            pltpu.HBM((4, PAD, BLOCK), bf16),
            pltpu.HBM((4, PAD, BLOCK), bf16),
        ),
        compiler_params=pltpu.CompilerParams(
            dimension_semantics=("arbitrary",), vmem_limit_bytes=48 << 20
        ),
        name="ready",
    )(tile_rows, tile_cols, counts, margins)


def tile_kernel(
    place, rows, part_ref, same_ref, other_ref, weight_ref, offset_ref, blank_ref, other_blank_ref,
    col_out_ref, keep_ref, give_ref,
    part, near, weights, offsets, col_block, row_terms, whole, col_out, sems, out_sems,
):
    slots = [rows[k] % COLS for k in range(TILES)]
    own = [slots[k] % 2 == place[0] % 2 for k in range(TILES)]
    fetch = [lax.rem(place[0] // 2 - slots[k] // 2 + 4, 4) for k in range(TILES)]
    leave = [lax.rem(slots[k] // 2 - place[0] // 2 + 4, 4) for k in range(TILES)]

    def near_move(k, ref=same_ref):
        return pltpu.make_async_copy(ref.at[fetch[k]], near.at[k], sems.at[k, 0])

    def part_move(k):
        return pltpu.make_async_copy(part_ref.at[:, k], part.at[k], sems.at[k, 1])

    def moves(k, c, width):
        cut = pl.ds(c * width, width)
        return [
            pltpu.make_async_copy(weight_ref.at[k, cut, :], weights.at[k, cut, :], sems.at[k, 2 + c]),
            pltpu.make_async_copy(offset_ref.at[k, cut, :], offsets.at[k, cut, :], sems.at[k, 4 + c]),
        ]

    def out_move(k):
        return pltpu.make_async_copy(col_out.at[k], col_out_ref.at[:, k], out_sems.at[k])

    widths = [FIRST] + [BLOCK] * (TILES - 1)
    for k in range(TILES):
        part_move(k).start()
        pl.when(own[k])(near_move(k).start)
        pl.when(jnp.logical_not(own[k]))(near_move(k, other_ref).start)
        for c in range(BLOCK // widths[k]):
            for move in moves(k, c, widths[k]):
                move.start()

    for t in range(TILES):
        part_move(t).wait()
        for s in range(PARTS):
            n, h = s // 2, s % 2
            col_block[t, h * HALF : (h + 1) * HALF, n * LANES : (n + 1) * LANES] = part[t, s]
        near_move(t).wait()
        term = None
        for c in range(BLOCK // widths[t]):
            cut = slice(c * widths[t], (c + 1) * widths[t])
            row_part = near[t, :, cut]
            scores = lax.dot_general(
                row_part, col_block[t], (((0,), (0,)), ((), ())), preferred_element_type=f32
            )
            for move in moves(t, c, widths[t]):
                move.wait()
            weight = weights[t, cut, :]
            residue = scores + offsets[t, cut, :]
            logistic = (0.5 * err_scale) + (0.5 * err_scale) * jnp.tanh(0.5 * residue)
            errors = jnp.where(weight > 0.0, weight * residue, logistic).astype(bf16)
            row_terms[t, :, cut] = lax.dot_general(
                col_block[t], errors, (((1,), (1,)), ((), ())), preferred_element_type=f32
            )
            piece = jnp.dot(row_part, errors, preferred_element_type=f32)
            term = piece if term is None else term + piece
        term = term.astype(bf16)
        for s in range(PARTS):
            n, h = s // 2, s % 2
            col_out[t, s] = term[h * HALF : (h + 1) * HALF, n * LANES : (n + 1) * LANES]
        out_move(t).start()

    fresh = [slots[0] >= 0, slots[1] != slots[0], (slots[2] != slots[0]) & (slots[2] != slots[1])]

    def sum_move(k, ref):
        return pltpu.make_async_copy(whole.at[k], ref.at[leave[k]], out_sems.at[TILES + k])

    for k in range(TILES):
        total = row_terms[k]
        for other in range(k + 1, TILES):
            same = jnp.where(slots[other] == slots[k], 1.0, 0.0)
            total = total + same * row_terms[other]
        whole[k] = total.astype(bf16)
    for k in range(TILES):
        pl.when(fresh[k] & own[k])(sum_move(k, keep_ref).start)
        pl.when(fresh[k] & jnp.logical_not(own[k]))(sum_move(k, give_ref).start)
    for k in range(TILES):
        pl.when(fresh[k])(sum_move(k, keep_ref).wait)
        out_move(k).wait()


def tile_terms(place, tile_rows, parts, same, other, weight, offset, blank, other_blank):
    quad = pltpu.HBM((4, PAD, BLOCK), bf16)
    return pl.pallas_call(
        tile_kernel,
        in_specs=[SMEM, SMEM] + [HBM] * 7,
        out_specs=[HBM] * 3,
        scratch_shapes=[
            pltpu.VMEM((TILES, PARTS, HALF, LANES), bf16),
            pltpu.VMEM((TILES, PAD, BLOCK), bf16),
            pltpu.VMEM((TILES, BLOCK, BLOCK), f32),
            pltpu.VMEM((TILES, BLOCK, BLOCK), f32),
            pltpu.VMEM((TILES, PAD, BLOCK), bf16),
            pltpu.VMEM((TILES, PAD, BLOCK), f32),
            pltpu.VMEM((TILES, PAD, BLOCK), bf16),
            pltpu.VMEM((TILES, PARTS, HALF, LANES), bf16),
            pltpu.SemaphoreType.DMA((TILES, 6)),
            pltpu.SemaphoreType.DMA((2 * TILES,)),
        ],
        out_shape=(pltpu.HBM((PARTS, TILES, HALF, LANES), bf16), quad, quad),
        input_output_aliases={7: 1, 8: 2},
        compiler_params=pltpu.CompilerParams(vmem_limit_bytes=60 << 20),
        name="tile_terms",
    )(place, tile_rows, parts, same, other, weight, offset, blank, other_blank)


def join_kernel(keep_ref, got_ref, *out_refs):
    for k in range(4):
        out_refs[k][...] = (keep_ref[k].astype(f32) + got_ref[k].astype(f32)).astype(bf16)


def join(keep, got):
    return pl.pallas_call(
        join_kernel,
        out_shape=[jax.ShapeDtypeStruct((PAD, BLOCK), bf16)] * 4,
        in_specs=[VMEM] * 2,
        compiler_params=pltpu.CompilerParams(vmem_limit_bytes=16 << 20),
        name="join",
    )(keep, got)


def owner_sum_kernel(asked, term_ref, out_ref, total):
    total[...] = jnp.zeros((PARTS, HALF, LANES), f32)
    for d in range(PARTS):
        for t in range(TILES):
            total[asked[d, t]] += term_ref[d, t].astype(f32)
    out_ref[...] = total[...].astype(bf16)


def owner_sum(asked, terms):
    return pl.pallas_call(
        owner_sum_kernel,
        out_shape=jax.ShapeDtypeStruct((PARTS, HALF, LANES), bf16),
        in_specs=[SMEM, VMEM],
        out_specs=VMEM,
        scratch_shapes=[pltpu.VMEM((PARTS, HALF, LANES), f32)],
        compiler_params=pltpu.CompilerParams(vmem_limit_bytes=12 << 20),
        name="owner_sum",
    )(asked, terms)


def adagrad(weights, history, gradient):
    grown = history + gradient * gradient
    return (weights - learn_rate * gradient / jnp.sqrt(grown), grown)


def col_update_kernel(emb_ref, acc_ref, grad_ref, new_emb_ref, new_acc_ref, held, new, sems, out_sems):
    edge = HALF * GROUPS
    cuts = [pl.ds(0, edge), pl.ds(edge, DIM * GROUPS - edge)]
    for h in range(2):
        for i, ref in enumerate((emb_ref, acc_ref)):
            pltpu.make_async_copy(ref.at[cuts[h]], held.at[i, cuts[h]], sems.at[i, h]).start()
    for h in range(2):
        for i, ref in enumerate((emb_ref, acc_ref)):
            pltpu.make_async_copy(ref.at[cuts[h]], held.at[i, cuts[h]], sems.at[i, h]).wait()
        length = HALF if h == 0 else DIM - HALF
        for n in range(GROUPS):
            rows = span(h * HALF, length, n)
            new[0, rows, :], new[1, rows, :] = adagrad(
                held[0, rows, :], held[1, rows, :], grad_ref[2 * n + h].astype(f32)[0:length]
            )
        for i, ref in enumerate((new_emb_ref, new_acc_ref)):
            pltpu.make_async_copy(new.at[i, cuts[h]], ref.at[cuts[h]], out_sems.at[i, h]).start()
    for h in range(2):
        for i, ref in enumerate((new_emb_ref, new_acc_ref)):
            pltpu.make_async_copy(new.at[i, cuts[h]], ref.at[cuts[h]], out_sems.at[i, h]).wait()


def col_update(emb, acc, grad):
    shape = jax.ShapeDtypeStruct((GROUPS * DIM, LANES), f32)
    new_emb, new_acc = pl.pallas_call(
        col_update_kernel,
        out_shape=(shape, shape),
        in_specs=[HBM, HBM, VMEM],
        out_specs=[HBM, HBM],
        scratch_shapes=[
            pltpu.VMEM((2, GROUPS * DIM, LANES), f32),
            pltpu.VMEM((2, GROUPS * DIM, LANES), f32),
            pltpu.SemaphoreType.DMA((2, 2)),
            pltpu.SemaphoreType.DMA((2, 2)),
        ],
        compiler_params=pltpu.CompilerParams(vmem_limit_bytes=12 << 20),
        name="col_update",
    )(emb, acc, grad)
    return new_emb.reshape(1, DIM, BLOCK), new_acc.reshape(1, DIM, BLOCK)


def row_update_kernel(emb_ref, acc_ref, *refs):
    grad_refs, (new_emb_ref, new_acc_ref) = refs[:4], refs[4:]
    for n in range(GROUPS):
        rows = span(0, DIM, n)
        cut = slice(n * LANES, (n + 1) * LANES)
        first, *others = [ref[:, cut].astype(f32)[0:DIM] for ref in grad_refs]
        grad = (first + others[0]) + (others[1] + others[2])
        new_emb_ref[rows, :], new_acc_ref[rows, :] = adagrad(emb_ref[rows, :], acc_ref[rows, :], grad)


def row_update(emb, acc, grads):
    shape = jax.ShapeDtypeStruct((GROUPS * DIM, LANES), f32)
    new_emb, new_acc = pl.pallas_call(
        row_update_kernel,
        out_shape=(shape, shape),
        in_specs=[VMEM] * 6,
        compiler_params=pltpu.CompilerParams(vmem_limit_bytes=16 << 20),
        name="row_update",
    )(emb, acc, *grads)
    return new_emb.reshape(1, DIM, BLOCK), new_acc.reshape(1, DIM, BLOCK)


def send_along_z(array, step):
    return lax.ppermute(array, "col", [(i, (i + 2 * step) % COLS) for i in range(COLS)])


def swap_cores(array):
    return lax.ppermute(array, "col", [(i, i ^ 1) for i in range(COLS)])


def body(row_emb, col_emb, row_acc, col_acc, marginal_log, tile_rows, tile_cols, counts):
    row_emb, col_emb, row_acc, col_acc = (
        array.reshape(GROUPS * DIM, LANES) for array in (row_emb, col_emb, row_acc, col_acc)
    )
    margins = marginal_log.reshape(-1, GROUPS, LANES)
    place = lax.axis_index("col").astype(jnp.int32).reshape(1)
    slices = cut_up(tile_cols, col_emb)
    row_low = lower(row_emb)
    held = lax.all_to_all(slices, "row", 0, 0, tiled=True)
    near = [row_low] + [send_along_z(row_low, step) for step in (1, 2, 3)]
    weight, offset, blank, other_blank = ready(tile_rows, tile_cols, counts, margins)
    picked, asked = pick(held)
    parts = lax.all_to_all(picked, "row", 0, 0, tiled=True)
    same = jnp.concatenate(near, axis=0)
    other = swap_cores(same)
    terms, keep, give = tile_terms(
        place, tile_rows, parts, same, other, weight, offset, blank, other_blank
    )
    got = swap_cores(give)
    terms = lax.all_to_all(terms, "row", 0, 0, tiled=True)
    grads = join(keep, got)
    grads = [grads[0]] + [send_along_z(grads[step], step) for step in (1, 2, 3)]
    sums = owner_sum(asked, terms)
    col_sum = lax.all_to_all(sums, "row", 0, 0, tiled=True)
    new_row_emb, new_row_acc = row_update(row_emb, row_acc, grads)
    new_col_emb, new_col_acc = col_update(col_emb, col_acc, col_sum)
    return (new_row_emb, new_col_emb, new_row_acc, new_col_acc)


def solution(mesh):
    block = P(("row", "col"), None, None)
    return jax.shard_map(
        body,
        mesh=mesh,
        in_specs=(block, block, block, block, P(), P(("row", "col")), P(("row", "col")), block),
        out_specs=(block, block, block, block),
        check_vma=False,
    )
```

```python
import jax
import jax.numpy as jnp
from jax import lax
from jax.experimental import pallas as pl
from jax.experimental.pallas import tpu as pltpu
from jax.sharding import PartitionSpec as P


err_scale = 0.03125
learn_rate = 0.1

DIM = 300
PAD = 304
HALF = 152
META = 160
BLOCK = 1024
LANES = 128
PARTS = 16
TILES = 3
COLS = 8
FIRST = 512
GROUPS = 8

f32 = jnp.float32
bf16 = jnp.bfloat16

SMEM = pl.BlockSpec(memory_space=pltpu.SMEM)
VMEM = pl.BlockSpec(memory_space=pltpu.VMEM)
HBM = pl.BlockSpec(memory_space=pl.ANY)


def in_hbm(array):
    return pltpu.with_memory_space_constraint(array, pltpu.HBM)


def span(first, length, n):
    return pl.ds(first * GROUPS + n, length, stride=GROUPS)


def cut_kernel(wanted, col_ref, slice_ref, col, sems):
    edge = HALF * GROUPS
    moves = [
        pltpu.make_async_copy(col_ref.at[:edge], col.at[:edge], sems.at[0]),
        pltpu.make_async_copy(col_ref.at[edge:], col.at[edge:], sems.at[1]),
    ]
    for move in moves:
        move.start()
    lane = lax.broadcasted_iota(jnp.int32, (8, LANES), 1)
    spot = lax.broadcasted_iota(jnp.int32, (8, LANES), 0)
    ask = [wanted[t] // COLS for t in range(TILES)]
    meta = jnp.where(lane == 0, ask[0], jnp.where(lane == 1, ask[1], ask[2])).astype(f32)
    moves[0].wait()
    for n in range(GROUPS):
        top = jnp.concatenate([col[span(0, HALF, n), :], meta], axis=0)
        slice_ref[2 * n] = top.astype(bf16)
    moves[1].wait()
    for n in range(GROUPS):
        last = pltpu.roll(col[span(DIM - 8, 8, n), :], 4, 0)
        last = jnp.where(spot < 4, last, 0.0)
        low = jnp.concatenate([col[span(HALF, DIM - 4 - HALF, n), :], last, meta], axis=0)
        slice_ref[2 * n + 1] = low.astype(bf16)


def cut_up(tile_cols, col_emb):
    return pl.pallas_call(
        cut_kernel,
        out_shape=jax.ShapeDtypeStruct((PARTS, META, LANES), bf16),
        in_specs=[SMEM, HBM],
        out_specs=VMEM,
        scratch_shapes=[pltpu.VMEM((DIM * GROUPS, LANES), f32), pltpu.SemaphoreType.DMA((2,))],
        compiler_params=pltpu.CompilerParams(vmem_limit_bytes=8 << 20),
        name="cut_up",
    )(in_hbm(tile_cols), in_hbm(col_emb))


def low_kernel(row_ref, low_ref):
    low_ref[0, 288:PAD, :] = jnp.zeros((16, BLOCK), bf16)
    for n in range(GROUPS):
        low_ref[0, 0:DIM, n * LANES : (n + 1) * LANES] = row_ref[span(0, DIM, n), :].astype(bf16)


def lower(row_emb):
    return pl.pallas_call(
        low_kernel,
        out_shape=jax.ShapeDtypeStruct((1, PAD, BLOCK), bf16),
        in_specs=[VMEM],
        out_specs=VMEM,
        compiler_params=pltpu.CompilerParams(vmem_limit_bytes=8 << 20),
        name="lower",
    )(row_emb)


def pick_kernel(held_ref, out_ref, meta_ref, picked, asked, sem, sems):
    for d in range(PARTS):
        meta_ref[d : d + 1, :] = held_ref[d, HALF:META, :].astype(f32)[0:1, :].astype(jnp.int32)
    move = pltpu.make_async_copy(meta_ref, asked, sem)
    move.start()
    move.wait()
    quarter = PARTS // 4
    moves = []
    for q in range(4):
        some = pl.ds(q * quarter, quarter)
        for d in range(q * quarter, (q + 1) * quarter):
            for t in range(TILES):
                picked[d, t] = held_ref[asked[d, t], 0:HALF, :]
        moves.append(pltpu.make_async_copy(picked.at[some], out_ref.at[some], sems.at[q]))
        moves[q].start()
    for move in moves:
        move.wait()


def pick(held):
    return pl.pallas_call(
        pick_kernel,
        out_shape=(
            pltpu.HBM((PARTS, TILES, HALF, LANES), bf16),
            jax.ShapeDtypeStruct((PARTS, LANES), jnp.int32),
        ),
        in_specs=[VMEM],
        out_specs=[HBM, VMEM],
        scratch_shapes=[
            pltpu.VMEM((PARTS, TILES, HALF, LANES), bf16),
            pltpu.SMEM((PARTS, LANES), jnp.int32),
            pltpu.SemaphoreType.DMA,
            pltpu.SemaphoreType.DMA((4,)),
        ],
        compiler_params=pltpu.CompilerParams(vmem_limit_bytes=8 << 20),
        name="pick",
    )(held)


def ready_kernel(
    rows, cols, count_ref, margin_ref, weight_ref, offset_ref, blank_ref, other_blank_ref,
    margin, zero, sems,
):
    t = pl.program_id(0)

    def margin_moves(k):
        return [
            pltpu.make_async_copy(margin_ref.at[rows[k]], margin.at[k, 0], sems.at[2 * k]),
            pltpu.make_async_copy(margin_ref.at[cols[k]], margin.at[k, 1], sems.at[2 * k + 1]),
        ]

    blank_moves = [
        pltpu.make_async_copy(zero, ref.at[s], sems.at[2 * TILES + 4 * i + s])
        for i, ref in enumerate((blank_ref, other_blank_ref))
        for s in range(4)
    ]

    @pl.when(t == 0)
    def _():
        for k in range(TILES):
            for move in margin_moves(k):
                move.start()
        zero[...] = jnp.zeros((PAD, BLOCK), bf16)
        for move in blank_moves:
            move.start()

    for move in margin_moves(t):
        move.wait()
    row_margin = jnp.transpose(margin[t, 0])
    col_margin = jnp.concatenate([margin[t, 1, n : n + 1, :] for n in range(GROUPS)], axis=1)
    for n in range(GROUPS):
        cut = slice(n * LANES, (n + 1) * LANES)
        counted = count_ref[0, cut, :].astype(f32)
        capped = jnp.maximum(counted, 1.0)
        offset_ref[0, cut, :] = (row_margin[:, n : n + 1] + col_margin) - jnp.log(capped)
        weight = (0.1 * err_scale) + (0.25 * err_scale) * (counted * lax.rsqrt(capped))
        weight_ref[0, cut, :] = jnp.where(counted > 0.0, weight, 0.0)

    @pl.when(t == TILES - 1)
    def _():
        for move in blank_moves:
            move.wait()


def ready(tile_rows, tile_cols, counts, margins):
    square = pl.BlockSpec((1, BLOCK, BLOCK), lambda t, *_: (t, 0, 0))
    grid_spec = pltpu.PrefetchScalarGridSpec(
        num_scalar_prefetch=2,
        grid=(TILES,),
        in_specs=[square, HBM],
        out_specs=[square, square, HBM, HBM],
        scratch_shapes=[
            pltpu.VMEM((TILES, 2, GROUPS, LANES), f32),
            pltpu.VMEM((PAD, BLOCK), bf16),
            pltpu.SemaphoreType.DMA((2 * TILES + 8,)),
        ],
    )
    return pl.pallas_call(
        ready_kernel,
        grid_spec=grid_spec,
        out_shape=(
            jax.ShapeDtypeStruct((TILES, BLOCK, BLOCK), f32),
            jax.ShapeDtypeStruct((TILES, BLOCK, BLOCK), f32),
            pltpu.HBM((4, PAD, BLOCK), bf16),
            pltpu.HBM((4, PAD, BLOCK), bf16),
        ),
        compiler_params=pltpu.CompilerParams(
            dimension_semantics=("arbitrary",), vmem_limit_bytes=48 << 20
        ),
        name="ready",
    )(tile_rows, tile_cols, counts, margins)


def tile_kernel(
    place, rows, part_ref, same_ref, other_ref, weight_ref, offset_ref, blank_ref, other_blank_ref,
    col_out_ref, keep_ref, give_ref,
    part, near, weights, offsets, col_block, row_terms, whole, col_out, sems, out_sems,
):
    slots = [rows[k] % COLS for k in range(TILES)]
    own = [slots[k] % 2 == place[0] % 2 for k in range(TILES)]
    fetch = [lax.rem(place[0] // 2 - slots[k] // 2 + 4, 4) for k in range(TILES)]
    leave = [lax.rem(slots[k] // 2 - place[0] // 2 + 4, 4) for k in range(TILES)]

    def near_move(k, ref=same_ref):
        return pltpu.make_async_copy(ref.at[fetch[k]], near.at[k], sems.at[k, 0])

    def part_move(k):
        return pltpu.make_async_copy(part_ref.at[:, k], part.at[k], sems.at[k, 1])

    def moves(k, c, width):
        cut = pl.ds(c * width, width)
        return [
            pltpu.make_async_copy(weight_ref.at[k, cut, :], weights.at[k, cut, :], sems.at[k, 2 + c]),
            pltpu.make_async_copy(offset_ref.at[k, cut, :], offsets.at[k, cut, :], sems.at[k, 4 + c]),
        ]

    def out_move(k):
        return pltpu.make_async_copy(col_out.at[k], col_out_ref.at[:, k], out_sems.at[k])

    widths = [FIRST] + [BLOCK] * (TILES - 1)
    for k in range(TILES):
        part_move(k).start()
        pl.when(own[k])(near_move(k).start)
        pl.when(jnp.logical_not(own[k]))(near_move(k, other_ref).start)
        for c in range(BLOCK // widths[k]):
            for move in moves(k, c, widths[k]):
                move.start()

    for t in range(TILES):
        part_move(t).wait()
        for s in range(PARTS):
            n, h = s // 2, s % 2
            col_block[t, h * HALF : (h + 1) * HALF, n * LANES : (n + 1) * LANES] = part[t, s]
        near_move(t).wait()
        term = None
        for c in range(BLOCK // widths[t]):
            cut = slice(c * widths[t], (c + 1) * widths[t])
            row_part = near[t, :, cut]
            scores = lax.dot_general(
                row_part, col_block[t], (((0,), (0,)), ((), ())), preferred_element_type=f32
            )
            for move in moves(t, c, widths[t]):
                move.wait()
            weight = weights[t, cut, :]
            residue = scores + offsets[t, cut, :]
            logistic = (0.5 * err_scale) + (0.5 * err_scale) * jnp.tanh(0.5 * residue)
            errors = jnp.where(weight > 0.0, weight * residue, logistic).astype(bf16)
            row_terms[t, :, cut] = lax.dot_general(
                col_block[t], errors, (((1,), (1,)), ((), ())), preferred_element_type=f32
            )
            piece = jnp.dot(row_part, errors, preferred_element_type=f32)
            term = piece if term is None else term + piece
        term = term.astype(bf16)
        for s in range(PARTS):
            n, h = s // 2, s % 2
            col_out[t, s] = term[h * HALF : (h + 1) * HALF, n * LANES : (n + 1) * LANES]
        out_move(t).start()

    fresh = [slots[0] >= 0, slots[1] != slots[0], (slots[2] != slots[0]) & (slots[2] != slots[1])]

    def sum_move(k, ref):
        return pltpu.make_async_copy(whole.at[k], ref.at[leave[k]], out_sems.at[TILES + k])

    for k in range(TILES):
        total = row_terms[k]
        for other in range(k + 1, TILES):
            same = jnp.where(slots[other] == slots[k], 1.0, 0.0)
            total = total + same * row_terms[other]
        whole[k] = total.astype(bf16)
    for k in range(TILES):
        pl.when(fresh[k] & own[k])(sum_move(k, keep_ref).start)
        pl.when(fresh[k] & jnp.logical_not(own[k]))(sum_move(k, give_ref).start)
    for k in range(TILES):
        pl.when(fresh[k])(sum_move(k, keep_ref).wait)
        out_move(k).wait()


def tile_terms(place, tile_rows, parts, same, other, weight, offset, blank, other_blank):
    quad = pltpu.HBM((4, PAD, BLOCK), bf16)
    return pl.pallas_call(
        tile_kernel,
        in_specs=[SMEM, SMEM] + [HBM] * 7,
        out_specs=[HBM] * 3,
        scratch_shapes=[
            pltpu.VMEM((TILES, PARTS, HALF, LANES), bf16),
            pltpu.VMEM((TILES, PAD, BLOCK), bf16),
            pltpu.VMEM((TILES, BLOCK, BLOCK), f32),
            pltpu.VMEM((TILES, BLOCK, BLOCK), f32),
            pltpu.VMEM((TILES, PAD, BLOCK), bf16),
            pltpu.VMEM((TILES, PAD, BLOCK), f32),
            pltpu.VMEM((TILES, PAD, BLOCK), bf16),
            pltpu.VMEM((TILES, PARTS, HALF, LANES), bf16),
            pltpu.SemaphoreType.DMA((TILES, 6)),
            pltpu.SemaphoreType.DMA((2 * TILES,)),
        ],
        out_shape=(pltpu.HBM((PARTS, TILES, HALF, LANES), bf16), quad, quad),
        input_output_aliases={7: 1, 8: 2},
        compiler_params=pltpu.CompilerParams(vmem_limit_bytes=60 << 20),
        name="tile_terms",
    )(place, tile_rows, in_hbm(parts), in_hbm(same), in_hbm(other), weight, offset, blank, other_blank)


def join_kernel(keep_ref, got_ref, *out_refs):
    for k in range(4):
        out_refs[k][...] = (keep_ref[k].astype(f32) + got_ref[k].astype(f32)).astype(bf16)


def join(keep, got):
    return pl.pallas_call(
        join_kernel,
        out_shape=[jax.ShapeDtypeStruct((PAD, BLOCK), bf16)] * 4,
        in_specs=[VMEM] * 2,
        compiler_params=pltpu.CompilerParams(vmem_limit_bytes=16 << 20),
        name="join",
    )(keep, got)


def owner_sum_kernel(asked, term_ref, out_ref, terms, total, sums, sems):
    quarter = PARTS // 4
    moves = []
    for q in range(4):
        some = pl.ds(q * quarter, quarter)
        moves.append(pltpu.make_async_copy(term_ref.at[some], terms.at[some], sems.at[q]))
        moves[q].start()
    total[...] = jnp.zeros((PARTS, HALF, LANES), f32)
    for q in range(4):
        moves[q].wait()
        for d in range(q * quarter, (q + 1) * quarter):
            for t in range(TILES):
                total[asked[d, t]] += terms[d, t].astype(f32)
    outs = []
    for q in range(4):
        some = pl.ds(q * quarter, quarter)
        sums[some] = total[some].astype(bf16)
        outs.append(pltpu.make_async_copy(sums.at[some], out_ref.at[some], sems.at[4 + q]))
        outs[q].start()
    for out in outs:
        out.wait()


def owner_sum(asked, terms):
    return pl.pallas_call(
        owner_sum_kernel,
        out_shape=pltpu.HBM((PARTS, HALF, LANES), bf16),
        in_specs=[SMEM, HBM],
        out_specs=HBM,
        scratch_shapes=[
            pltpu.VMEM((PARTS, TILES, HALF, LANES), bf16),
            pltpu.VMEM((PARTS, HALF, LANES), f32),
            pltpu.VMEM((PARTS, HALF, LANES), bf16),
            pltpu.SemaphoreType.DMA((8,)),
        ],
        compiler_params=pltpu.CompilerParams(vmem_limit_bytes=12 << 20),
        name="owner_sum",
    )(asked, in_hbm(terms))


def adagrad(weights, history, gradient):
    grown = history + gradient * gradient
    return (weights - learn_rate * gradient / jnp.sqrt(grown), grown)


def col_update_kernel(emb_ref, acc_ref, grad_ref, new_emb_ref, new_acc_ref, held, new, sems, out_sems):
    edge = HALF * GROUPS
    cuts = [pl.ds(0, edge), pl.ds(edge, DIM * GROUPS - edge)]
    for h in range(2):
        for i, ref in enumerate((emb_ref, acc_ref)):
            pltpu.make_async_copy(ref.at[cuts[h]], held.at[i, cuts[h]], sems.at[i, h]).start()
    for h in range(2):
        for i, ref in enumerate((emb_ref, acc_ref)):
            pltpu.make_async_copy(ref.at[cuts[h]], held.at[i, cuts[h]], sems.at[i, h]).wait()
        length = HALF if h == 0 else DIM - HALF
        for n in range(GROUPS):
            rows = span(h * HALF, length, n)
            new[0, rows, :], new[1, rows, :] = adagrad(
                held[0, rows, :], held[1, rows, :], grad_ref[2 * n + h].astype(f32)[0:length]
            )
        for i, ref in enumerate((new_emb_ref, new_acc_ref)):
            pltpu.make_async_copy(new.at[i, cuts[h]], ref.at[cuts[h]], out_sems.at[i, h]).start()
    for h in range(2):
        for i, ref in enumerate((new_emb_ref, new_acc_ref)):
            pltpu.make_async_copy(new.at[i, cuts[h]], ref.at[cuts[h]], out_sems.at[i, h]).wait()


def col_update(emb, acc, grad):
    shape = jax.ShapeDtypeStruct((GROUPS * DIM, LANES), f32)
    new_emb, new_acc = pl.pallas_call(
        col_update_kernel,
        out_shape=(shape, shape),
        in_specs=[HBM, HBM, VMEM],
        out_specs=[HBM, HBM],
        scratch_shapes=[
            pltpu.VMEM((2, GROUPS * DIM, LANES), f32),
            pltpu.VMEM((2, GROUPS * DIM, LANES), f32),
            pltpu.SemaphoreType.DMA((2, 2)),
            pltpu.SemaphoreType.DMA((2, 2)),
        ],
        compiler_params=pltpu.CompilerParams(vmem_limit_bytes=12 << 20),
        name="col_update",
    )(in_hbm(emb), in_hbm(acc), grad)
    return new_emb.reshape(1, DIM, BLOCK), new_acc.reshape(1, DIM, BLOCK)


def row_update_kernel(emb_ref, acc_ref, *refs):
    grad_refs, (new_emb_ref, new_acc_ref) = refs[:4], refs[4:]
    for n in range(GROUPS):
        rows = span(0, DIM, n)
        cut = slice(n * LANES, (n + 1) * LANES)
        first, *others = [ref[:, cut].astype(f32)[0:DIM] for ref in grad_refs]
        grad = (first + others[0]) + (others[1] + others[2])
        new_emb_ref[rows, :], new_acc_ref[rows, :] = adagrad(emb_ref[rows, :], acc_ref[rows, :], grad)


def row_update(emb, acc, grads):
    shape = jax.ShapeDtypeStruct((GROUPS * DIM, LANES), f32)
    new_emb, new_acc = pl.pallas_call(
        row_update_kernel,
        out_shape=(shape, shape),
        in_specs=[VMEM] * 6,
        compiler_params=pltpu.CompilerParams(vmem_limit_bytes=16 << 20),
        name="row_update",
    )(emb, acc, *grads)
    return new_emb.reshape(1, DIM, BLOCK), new_acc.reshape(1, DIM, BLOCK)


def send_along_z(array, step):
    return lax.ppermute(array, "col", [(i, (i + 2 * step) % COLS) for i in range(COLS)])


def swap_cores(array):
    return lax.ppermute(array, "col", [(i, i ^ 1) for i in range(COLS)])


def body(row_emb, col_emb, row_acc, col_acc, marginal_log, tile_rows, tile_cols, counts):
    row_emb, col_emb, row_acc, col_acc = (
        array.reshape(GROUPS * DIM, LANES) for array in (row_emb, col_emb, row_acc, col_acc)
    )
    margins = marginal_log.reshape(-1, GROUPS, LANES)
    place = lax.axis_index("col").astype(jnp.int32).reshape(1)
    slices = cut_up(tile_cols, col_emb)
    row_low = lower(row_emb)
    held = lax.all_to_all(slices, "row", 0, 0, tiled=True)
    near = [row_low] + [send_along_z(row_low, step) for step in (1, 2, 3)]
    weight, offset, blank, other_blank = ready(tile_rows, tile_cols, counts, margins)
    picked, asked = pick(held)
    parts = lax.all_to_all(picked, "row", 0, 0, tiled=True)
    same = jnp.concatenate(near, axis=0)
    other = swap_cores(same)
    terms, keep, give = tile_terms(
        place, tile_rows, parts, same, other, weight, offset, blank, other_blank
    )
    got = swap_cores(give)
    terms = lax.all_to_all(terms, "row", 0, 0, tiled=True)
    grads = join(keep, got)
    grads = [grads[0]] + [send_along_z(grads[step], step) for step in (1, 2, 3)]
    sums = owner_sum(asked, terms)
    col_sum = lax.all_to_all(sums, "row", 0, 0, tiled=True)
    new_row_emb, new_row_acc = row_update(row_emb, row_acc, grads)
    new_col_emb, new_col_acc = col_update(col_emb, col_acc, col_sum)
    return (new_row_emb, new_col_emb, new_row_acc, new_col_acc)


def solution(mesh):
    block = P(("row", "col"), None, None)
    return jax.shard_map(
        body,
        mesh=mesh,
        in_specs=(block, block, block, block, P(), P(("row", "col")), P(("row", "col")), block),
        out_specs=(block, block, block, block),
        check_vma=False,
    )
```

```python
import functools

import jax
import jax.numpy as jnp
from jax import lax
from jax.experimental import pallas as pl
from jax.experimental.pallas import tpu as pltpu
from jax.sharding import PartitionSpec as P


err_scale = 0.03125
learn_rate = 0.1

DIM = 300
PAD = 304
HALF = 152
META = 160
BLOCK = 1024
LANES = 128
PARTS = 16
TILES = 3
COLS = 8
FIRST = 512
GROUPS = 8
ROW_CUT = 160

f32 = jnp.float32
bf16 = jnp.bfloat16

SMEM = pl.BlockSpec(memory_space=pltpu.SMEM)
VMEM = pl.BlockSpec(memory_space=pltpu.VMEM)
HBM = pl.BlockSpec(memory_space=pl.ANY)


def in_vmem(array):
    return pltpu.with_memory_space_constraint(array, pltpu.VMEM)


def in_hbm(array):
    return pltpu.with_memory_space_constraint(array, pltpu.HBM)


def span(first, length, n):
    return pl.ds(first * GROUPS + n, length, stride=GROUPS)


def cut_kernel(wanted, col_ref, slice_ref, col, cut, sems):
    edge = HALF * GROUPS
    moves = [
        pltpu.make_async_copy(col_ref.at[:edge], col.at[:edge], sems.at[0]),
        pltpu.make_async_copy(col_ref.at[edge:], col.at[edge:], sems.at[1]),
    ]
    for move in moves:
        move.start()
    lane = lax.broadcasted_iota(jnp.int32, (8, LANES), 1)
    spot = lax.broadcasted_iota(jnp.int32, (8, LANES), 0)
    ask = [wanted[t] // COLS for t in range(TILES)]
    meta = jnp.where(lane == 0, ask[0], jnp.where(lane == 1, ask[1], ask[2])).astype(f32)
    moves[0].wait()
    for n in range(GROUPS):
        top = jnp.concatenate([col[span(0, HALF, n), :], meta], axis=0)
        cut[0, n] = top.astype(bf16)
    outs = [pltpu.make_async_copy(cut.at[h], slice_ref.at[:, h], sems.at[2 + h]) for h in range(2)]
    outs[0].start()
    moves[1].wait()
    for n in range(GROUPS):
        last = pltpu.roll(col[span(DIM - 8, 8, n), :], 4, 0)
        last = jnp.where(spot < 4, last, 0.0)
        low = jnp.concatenate([col[span(HALF, DIM - 4 - HALF, n), :], last, meta], axis=0)
        cut[1, n] = low.astype(bf16)
    outs[1].start()
    for out in outs:
        out.wait()


def cut_up(tile_cols, col_emb):
    return pl.pallas_call(
        cut_kernel,
        out_shape=pltpu.HBM((GROUPS, 2, META, LANES), bf16),
        in_specs=[SMEM, HBM],
        out_specs=HBM,
        scratch_shapes=[
            pltpu.VMEM((DIM * GROUPS, LANES), f32),
            pltpu.VMEM((2, GROUPS, META, LANES), bf16),
            pltpu.SemaphoreType.DMA((4,)),
        ],
        compiler_params=pltpu.CompilerParams(vmem_limit_bytes=8 << 20),
        name="cut_up",
    )(in_hbm(tile_cols), in_hbm(col_emb)).reshape(PARTS, META, LANES)


def low_kernel(row_ref, low_ref):
    low_ref[0, 288:PAD, :] = jnp.zeros((16, BLOCK), bf16)
    for n in range(GROUPS):
        low_ref[0, 0:DIM, n * LANES : (n + 1) * LANES] = row_ref[span(0, DIM, n), :].astype(bf16)


def lower(row_emb):
    return pl.pallas_call(
        low_kernel,
        out_shape=jax.ShapeDtypeStruct((1, PAD, BLOCK), bf16),
        in_specs=[VMEM],
        out_specs=VMEM,
        compiler_params=pltpu.CompilerParams(vmem_limit_bytes=8 << 20),
        name="lower",
    )(row_emb)


def pick_kernel(held_ref, out_ref, meta_ref, picked, asked, sem, sems):
    for d in range(PARTS):
        meta_ref[d : d + 1, :] = held_ref[d, HALF:META, :].astype(f32)[0:1, :].astype(jnp.int32)
    move = pltpu.make_async_copy(meta_ref, asked, sem)
    move.start()
    move.wait()
    quarter = PARTS // 4
    moves = []
    for q in range(4):
        some = pl.ds(q * quarter, quarter)
        for d in range(q * quarter, (q + 1) * quarter):
            for t in range(TILES):
                picked[d, t] = held_ref[asked[d, t], 0:HALF, :]
        moves.append(pltpu.make_async_copy(picked.at[some], out_ref.at[some], sems.at[q]))
        moves[q].start()
    for move in moves:
        move.wait()


def pick(held):
    return pl.pallas_call(
        pick_kernel,
        out_shape=(
            pltpu.HBM((PARTS, TILES, HALF, LANES), bf16),
            jax.ShapeDtypeStruct((PARTS, LANES), jnp.int32),
        ),
        in_specs=[VMEM],
        out_specs=[HBM, VMEM],
        scratch_shapes=[
            pltpu.VMEM((PARTS, TILES, HALF, LANES), bf16),
            pltpu.SMEM((PARTS, LANES), jnp.int32),
            pltpu.SemaphoreType.DMA,
            pltpu.SemaphoreType.DMA((4,)),
        ],
        compiler_params=pltpu.CompilerParams(vmem_limit_bytes=8 << 20),
        name="pick",
    )(held)


def ready_kernel(base, count, rows, cols, count_ref, margin_ref, weight_ref, offset_ref, *refs):
    blank_refs, (margin, zero, sems) = refs[:-3], refs[-3:]
    t = pl.program_id(0)

    def margin_moves(k):
        return [
            pltpu.make_async_copy(margin_ref.at[rows[base + k]], margin.at[k, 0], sems.at[2 * k]),
            pltpu.make_async_copy(margin_ref.at[cols[base + k]], margin.at[k, 1], sems.at[2 * k + 1]),
        ]

    blank_moves = [
        pltpu.make_async_copy(zero, ref.at[s], sems.at[2 * TILES + 4 * i + s])
        for i, ref in enumerate(blank_refs)
        for s in range(4)
    ]

    @pl.when(t == 0)
    def _():
        for k in range(count):
            for move in margin_moves(k):
                move.start()
        if blank_refs:
            zero[...] = jnp.zeros((PAD, BLOCK), bf16)
        for move in blank_moves:
            move.start()

    for move in margin_moves(t):
        move.wait()
    row_margin = jnp.transpose(margin[t, 0])
    col_margin = jnp.concatenate([margin[t, 1, n : n + 1, :] for n in range(GROUPS)], axis=1)
    for n in range(GROUPS):
        cut = slice(n * LANES, (n + 1) * LANES)
        counted = count_ref[0, cut, :].astype(f32)
        capped = jnp.maximum(counted, 1.0)
        offset_ref[0, cut, :] = (row_margin[:, n : n + 1] + col_margin) - jnp.log(capped)
        weight = (0.1 * err_scale) + (0.25 * err_scale) * (counted * lax.rsqrt(capped))
        weight_ref[0, cut, :] = jnp.where(counted > 0.0, weight, 0.0)

    if blank_refs:

        @pl.when(t == count - 1)
        def _():
            for move in blank_moves:
                move.wait()


def ready(base, count, blanks, tile_rows, tile_cols, counts, margins):
    square = pl.BlockSpec((1, BLOCK, BLOCK), lambda t, *_: (t, 0, 0))
    grid_spec = pltpu.PrefetchScalarGridSpec(
        num_scalar_prefetch=2,
        grid=(count,),
        in_specs=[pl.BlockSpec((1, BLOCK, BLOCK), lambda t, *_: (base + t, 0, 0)), HBM],
        out_specs=[square, square] + [HBM] * blanks,
        scratch_shapes=[
            pltpu.VMEM((count, 2, GROUPS, LANES), f32),
            pltpu.VMEM((PAD, BLOCK), bf16),
            pltpu.SemaphoreType.DMA((2 * TILES + 8,)),
        ],
    )
    return pl.pallas_call(
        functools.partial(ready_kernel, base, count),
        grid_spec=grid_spec,
        out_shape=[pltpu.HBM((count, BLOCK, BLOCK), f32)] * 2
        + [pltpu.HBM((4, PAD, BLOCK), bf16)] * blanks,
        compiler_params=pltpu.CompilerParams(
            dimension_semantics=("arbitrary",), vmem_limit_bytes=48 << 20
        ),
    )(tile_rows, tile_cols, counts, margins)


def tile_kernel(
    place, rows, part_ref, same_ref, other_ref, first_weight_ref, first_offset_ref,
    weight_ref, offset_ref, blank_ref, other_blank_ref,
    col_out_ref, keep_ref, give_ref,
    part, near, weights, offsets, col_block, row_terms, whole, col_out, sems, out_sems,
):
    slots = [rows[k] % COLS for k in range(TILES)]
    own = [slots[k] % 2 == place[0] % 2 for k in range(TILES)]
    fetch = [lax.rem(place[0] // 2 - slots[k] // 2 + 4, 4) for k in range(TILES)]
    leave = [lax.rem(slots[k] // 2 - place[0] // 2 + 4, 4) for k in range(TILES)]

    def near_move(k, ref=same_ref):
        return pltpu.make_async_copy(ref.at[fetch[k]], near.at[k], sems.at[k, 0])

    def part_move(k):
        return pltpu.make_async_copy(part_ref.at[:, k], part.at[k], sems.at[k, 1])

    def moves(k, c, width):
        cut = pl.ds(c * width, width)
        refs, at = (first_weight_ref, first_offset_ref), k
        if k > 0:
            refs, at = (weight_ref, offset_ref), k - 1
        return [
            pltpu.make_async_copy(refs[0].at[at, cut, :], weights.at[k, cut, :], sems.at[k, 2 + c]),
            pltpu.make_async_copy(refs[1].at[at, cut, :], offsets.at[k, cut, :], sems.at[k, 4 + c]),
        ]

    def out_move(k):
        return pltpu.make_async_copy(col_out.at[k], col_out_ref.at[:, k], out_sems.at[k])

    widths = [FIRST] + [BLOCK] * (TILES - 1)
    for k in range(TILES):
        part_move(k).start()
        pl.when(own[k])(near_move(k).start)
        pl.when(jnp.logical_not(own[k]))(near_move(k, other_ref).start)
        for c in range(BLOCK // widths[k]):
            for move in moves(k, c, widths[k]):
                move.start()

    for t in range(TILES):
        part_move(t).wait()
        for s in range(PARTS):
            n, h = s // 2, s % 2
            col_block[t, h * HALF : (h + 1) * HALF, n * LANES : (n + 1) * LANES] = part[t, s]
        near_move(t).wait()
        term = None
        for c in range(BLOCK // widths[t]):
            cut = slice(c * widths[t], (c + 1) * widths[t])
            row_part = near[t, :, cut]
            scores = lax.dot_general(
                row_part, col_block[t], (((0,), (0,)), ((), ())), preferred_element_type=f32
            )
            for move in moves(t, c, widths[t]):
                move.wait()
            weight = weights[t, cut, :]
            residue = scores + offsets[t, cut, :]
            logistic = (0.5 * err_scale) + (0.5 * err_scale) * jnp.tanh(0.5 * residue)
            errors = jnp.where(weight > 0.0, weight * residue, logistic).astype(bf16)
            row_terms[t, :, cut] = lax.dot_general(
                col_block[t], errors, (((1,), (1,)), ((), ())), preferred_element_type=f32
            )
            piece = jnp.dot(row_part, errors, preferred_element_type=f32)
            term = piece if term is None else term + piece
        term = term.astype(bf16)
        for s in range(PARTS):
            n, h = s // 2, s % 2
            col_out[t, s] = term[h * HALF : (h + 1) * HALF, n * LANES : (n + 1) * LANES]
        out_move(t).start()

    fresh = [slots[0] >= 0, slots[1] != slots[0], (slots[2] != slots[0]) & (slots[2] != slots[1])]

    def sum_move(k, ref):
        return pltpu.make_async_copy(whole.at[k], ref.at[leave[k]], out_sems.at[TILES + k])

    for k in range(TILES):
        total = row_terms[k]
        for other in range(k + 1, TILES):
            same = jnp.where(slots[other] == slots[k], 1.0, 0.0)
            total = total + same * row_terms[other]
        whole[k] = total.astype(bf16)
    for k in range(TILES):
        pl.when(fresh[k] & own[k])(sum_move(k, keep_ref).start)
        pl.when(fresh[k] & jnp.logical_not(own[k]))(sum_move(k, give_ref).start)
    for k in range(TILES):
        pl.when(fresh[k])(sum_move(k, keep_ref).wait)
        out_move(k).wait()


def tile_terms(place, tile_rows, parts, same, other, begun, rest):
    quad = pltpu.HBM((4, PAD, BLOCK), bf16)
    return pl.pallas_call(
        tile_kernel,
        in_specs=[SMEM, SMEM] + [HBM] * 9,
        out_specs=[HBM] * 3,
        scratch_shapes=[
            pltpu.VMEM((TILES, PARTS, HALF, LANES), bf16),
            pltpu.VMEM((TILES, PAD, BLOCK), bf16),
            pltpu.VMEM((TILES, BLOCK, BLOCK), f32),
            pltpu.VMEM((TILES, BLOCK, BLOCK), f32),
            pltpu.VMEM((TILES, PAD, BLOCK), bf16),
            pltpu.VMEM((TILES, PAD, BLOCK), f32),
            pltpu.VMEM((TILES, PAD, BLOCK), bf16),
            pltpu.VMEM((TILES, PARTS, HALF, LANES), bf16),
            pltpu.SemaphoreType.DMA((TILES, 6)),
            pltpu.SemaphoreType.DMA((2 * TILES,)),
        ],
        out_shape=(pltpu.HBM((PARTS, TILES, HALF, LANES), bf16), quad, quad),
        input_output_aliases={9: 1, 10: 2},
        compiler_params=pltpu.CompilerParams(vmem_limit_bytes=60 << 20),
        name="tile_terms",
    )(place, tile_rows, in_hbm(parts), in_hbm(same), in_hbm(other), *begun, *rest)


def settle_kernel(array_ref, out_ref):
    del array_ref, out_ref


def settle(array):
    return pl.pallas_call(
        settle_kernel,
        out_shape=pltpu.HBM(array.shape, array.dtype),
        in_specs=[HBM],
        out_specs=HBM,
        input_output_aliases={0: 0},
        name="settle",
    )(in_hbm(array))


def join_kernel(keep_ref, got_ref, *refs):
    out_refs, (keep, got, sums, sems) = refs[:4], refs[4:]
    order = (1, 2, 3, 0)
    moves = [
        [
            pltpu.make_async_copy(keep_ref.at[k], keep.at[k], sems.at[0, k]),
            pltpu.make_async_copy(got_ref.at[k], got.at[k], sems.at[1, k]),
        ]
        for k in range(4)
    ]
    outs = [pltpu.make_async_copy(sums.at[k], out_refs[k], sems.at[2, k]) for k in range(4)]
    for k in order:
        for move in moves[k]:
            move.start()
    for k in order:
        for move in moves[k]:
            move.wait()
        sums[k] = (keep[k].astype(f32) + got[k].astype(f32)).astype(bf16)
        outs[k].start()
    for out in outs:
        out.wait()


def join(keep, got):
    quad = pltpu.VMEM((4, PAD, BLOCK), bf16)
    return pl.pallas_call(
        join_kernel,
        out_shape=[pltpu.HBM((PAD, BLOCK), bf16)] * 4,
        in_specs=[HBM] * 2,
        out_specs=[HBM] * 4,
        scratch_shapes=[quad, quad, quad, pltpu.SemaphoreType.DMA((3, 4))],
        compiler_params=pltpu.CompilerParams(vmem_limit_bytes=16 << 20),
        name="join",
    )(in_hbm(keep), got)


def owner_sum_kernel(asked, term_ref, out_ref, total, sums, sems):
    quarter = PARTS // 4
    total[...] = jnp.zeros((PARTS, HALF, LANES), f32)
    for d in range(PARTS):
        for t in range(TILES):
            total[asked[d, t]] += term_ref[d, t].astype(f32)
    outs = []
    for q in range(4):
        some = pl.ds(q * quarter, quarter)
        sums[some] = total[some].astype(bf16)
        outs.append(pltpu.make_async_copy(sums.at[some], out_ref.at[some], sems.at[q]))
        outs[q].start()
    for out in outs:
        out.wait()


def owner_sum(asked, terms):
    return pl.pallas_call(
        owner_sum_kernel,
        out_shape=pltpu.HBM((PARTS, HALF, LANES), bf16),
        in_specs=[SMEM, VMEM],
        out_specs=HBM,
        scratch_shapes=[
            pltpu.VMEM((PARTS, HALF, LANES), f32),
            pltpu.VMEM((PARTS, HALF, LANES), bf16),
            pltpu.SemaphoreType.DMA((4,)),
        ],
        compiler_params=pltpu.CompilerParams(vmem_limit_bytes=12 << 20),
        name="owner_sum",
    )(asked, in_vmem(terms))


def adagrad(weights, history, gradient):
    grown = history + gradient * gradient
    return (weights - learn_rate * gradient / jnp.sqrt(grown), grown)


def col_update_kernel(emb_ref, acc_ref, grad_ref, new_emb_ref, new_acc_ref, held, new, sems, out_sems):
    edge = HALF * GROUPS
    cuts = [pl.ds(0, edge), pl.ds(edge, DIM * GROUPS - edge)]
    for h in range(2):
        for i, ref in enumerate((emb_ref, acc_ref)):
            pltpu.make_async_copy(ref.at[cuts[h]], held.at[i, cuts[h]], sems.at[i, h]).start()
    for h in range(2):
        for i, ref in enumerate((emb_ref, acc_ref)):
            pltpu.make_async_copy(ref.at[cuts[h]], held.at[i, cuts[h]], sems.at[i, h]).wait()
        length = HALF if h == 0 else DIM - HALF
        for n in range(GROUPS):
            rows = span(h * HALF, length, n)
            new[0, rows, :], new[1, rows, :] = adagrad(
                held[0, rows, :], held[1, rows, :], grad_ref[2 * n + h].astype(f32)[0:length]
            )
        for i, ref in enumerate((new_emb_ref, new_acc_ref)):
            pltpu.make_async_copy(new.at[i, cuts[h]], ref.at[cuts[h]], out_sems.at[i, h]).start()
    for h in range(2):
        for i, ref in enumerate((new_emb_ref, new_acc_ref)):
            pltpu.make_async_copy(new.at[i, cuts[h]], ref.at[cuts[h]], out_sems.at[i, h]).wait()


def col_update(emb, acc, grad):
    shape = jax.ShapeDtypeStruct((GROUPS * DIM, LANES), f32)
    new_emb, new_acc = pl.pallas_call(
        col_update_kernel,
        out_shape=(shape, shape),
        in_specs=[HBM, HBM, VMEM],
        out_specs=[HBM, HBM],
        scratch_shapes=[
            pltpu.VMEM((2, GROUPS * DIM, LANES), f32),
            pltpu.VMEM((2, GROUPS * DIM, LANES), f32),
            pltpu.SemaphoreType.DMA((2, 2)),
            pltpu.SemaphoreType.DMA((2, 2)),
        ],
        compiler_params=pltpu.CompilerParams(vmem_limit_bytes=12 << 20),
        name="col_update",
    )(in_hbm(emb), in_hbm(acc), grad)
    return new_emb.reshape(1, DIM, BLOCK), new_acc.reshape(1, DIM, BLOCK)


def row_update_kernel(emb_ref, acc_ref, *refs):
    grad_refs, (new_emb_ref, new_acc_ref), (held, grad, new, sems, out_sems) = (
        refs[:4], refs[4:6], refs[6:],
    )
    firsts, edge = (0, ROW_CUT), (ROW_CUT, DIM - ROW_CUT)
    cuts = [pl.ds(first * GROUPS, length * GROUPS) for first, length in zip(firsts, edge)]
    grad_cuts = [pl.ds(0, ROW_CUT), pl.ds(ROW_CUT, PAD - ROW_CUT)]
    moves = [
        [
            pltpu.make_async_copy(ref.at[cuts[h]], held.at[i, cuts[h]], sems.at[i, h])
            for i, ref in enumerate((emb_ref, acc_ref))
        ]
        + [
            pltpu.make_async_copy(ref.at[grad_cuts[h]], grad.at[i, grad_cuts[h]], sems.at[2 + i, h])
            for i, ref in enumerate(grad_refs)
        ]
        for h in range(2)
    ]
    outs = [
        [
            pltpu.make_async_copy(new.at[i, cuts[h]], ref.at[cuts[h]], out_sems.at[i, h])
            for i, ref in enumerate((new_emb_ref, new_acc_ref))
        ]
        for h in range(2)
    ]
    for h in range(2):
        for move in moves[h]:
            move.start()
    for h in range(2):
        for move in moves[h]:
            move.wait()
        for n in range(GROUPS):
            rows = span(firsts[h], edge[h], n)
            cut = slice(n * LANES, (n + 1) * LANES)
            parts = [grad[i, grad_cuts[h], cut].astype(f32)[0 : edge[h]] for i in range(4)]
            total = (parts[0] + parts[1]) + (parts[2] + parts[3])
            new[0, rows, :], new[1, rows, :] = adagrad(held[0, rows, :], held[1, rows, :], total)
        for out in outs[h]:
            out.start()
    for h in range(2):
        for out in outs[h]:
            out.wait()


def row_update(emb, acc, grads):
    shape = jax.ShapeDtypeStruct((GROUPS * DIM, LANES), f32)
    new_emb, new_acc = pl.pallas_call(
        row_update_kernel,
        out_shape=(shape, shape),
        in_specs=[HBM] * 6,
        out_specs=[HBM, HBM],
        scratch_shapes=[
            pltpu.VMEM((2, GROUPS * DIM, LANES), f32),
            pltpu.VMEM((4, PAD, BLOCK), bf16),
            pltpu.VMEM((2, GROUPS * DIM, LANES), f32),
            pltpu.SemaphoreType.DMA((6, 2)),
            pltpu.SemaphoreType.DMA((2, 2)),
        ],
        compiler_params=pltpu.CompilerParams(vmem_limit_bytes=16 << 20),
        name="row_update",
    )(in_hbm(emb), in_hbm(acc), in_hbm(grads[0]), *grads[1:])
    return new_emb.reshape(1, DIM, BLOCK), new_acc.reshape(1, DIM, BLOCK)


def send_along_z(array, step):
    return lax.ppermute(array, "col", [(i, (i + 2 * step) % COLS) for i in range(COLS)])


def swap_cores(array):
    return lax.ppermute(array, "col", [(i, i ^ 1) for i in range(COLS)])


def body(row_emb, col_emb, row_acc, col_acc, marginal_log, tile_rows, tile_cols, counts):
    row_emb, col_emb, row_acc, col_acc = (
        array.reshape(GROUPS * DIM, LANES) for array in (row_emb, col_emb, row_acc, col_acc)
    )
    margins = marginal_log.reshape(-1, GROUPS, LANES)
    place = lax.axis_index("col").astype(jnp.int32).reshape(1)
    slices = cut_up(tile_cols, col_emb)
    row_low = lower(row_emb)
    held = lax.all_to_all(slices, "row", 0, 0, tiled=True)
    near = [row_low] + [send_along_z(row_low, step) for step in (1, 2, 3)]
    begun = ready(0, 1, 0, tile_rows, tile_cols, counts, margins)
    rest = ready(1, TILES - 1, 2, tile_rows, tile_cols, counts, margins)
    picked, asked = pick(held)
    parts = lax.all_to_all(picked, "row", 0, 0, tiled=True)
    same = jnp.concatenate(near, axis=0)
    other = swap_cores(same)
    other = settle(other)
    terms, keep, give = tile_terms(place, tile_rows, parts, same, other, begun, rest)
    got = swap_cores(give)
    terms = lax.all_to_all(terms, "row", 0, 0, tiled=True)
    grads = join(keep, got)
    grads = [grads[0]] + [send_along_z(grads[step], step) for step in (1, 2, 3)]
    sums = owner_sum(asked, terms)
    col_sum = lax.all_to_all(sums, "row", 0, 0, tiled=True)
    new_row_emb, new_row_acc = row_update(row_emb, row_acc, grads)
    new_col_emb, new_col_acc = col_update(col_emb, col_acc, col_sum)
    return (new_row_emb, new_col_emb, new_row_acc, new_col_acc)


def solution(mesh):
    block = P(("row", "col"), None, None)
    return jax.shard_map(
        body,
        mesh=mesh,
        in_specs=(block, block, block, block, P(), P(("row", "col")), P(("row", "col")), block),
        out_specs=(block, block, block, block),
        check_vma=False,
    )
```
